256 devices in a mesh: group: 16 (over z_lo, x), ingroup: 16 (over y, z_hi, core).
Axes of the slice: x: 4, y: 4, z: 8 (z_hi: 2, z_lo: 4; z = z_hi * 4 + z_lo), core: 2. Of those that a mesh axis runs over, the one named last changes fastest.
Arguments:
- inputs: bfloat16 [16, 16, 6144], P(None, 'ingroup', 'group'), may hold values from -14 to 14
- targets: bfloat16 [16, 16, 6144], P(None, 'ingroup', 'group'), may hold values from -4 to 4
- w_in: float32 [6144, 24576], P('group', 'ingroup'), may hold values from -2 to 2
- w_out: float32 [24576, 6144], P('ingroup', 'group'), may hold values from -2 to 2
Outputs:
- grad_in: float32 [6144, 24576], P('group', 'ingroup')
- grad_out: float32 [24576, 6144], P('ingroup', 'group')
The draws below stay inside these ranges and needn't reach their ends.
All inputs are finite; a program needn't handle non-finite values.
Results may differ from the reference program's by a relative error of at most 0.0052.
Values may be sent and summed in bfloat16 or wider, within the bound.
No kernel may reach another device: no remote copies, remote signals or barrier semaphores. Data moves between devices by JAX's collectives and lax.ppermute only.
A program may use at most 128 MiB of HBM per device.

```python
import math
import jax
import jax.numpy as jnp
from jax import lax

D = 6144
FF = 24576
GROUP_TOKENS = 16
N_GROUP = 16


def draw_inputs(key, part):
    first_key, second_key = jax.random.split(key, 2)
    position = jnp.arange(D, dtype=jnp.float32) / D
    jitter = jax.random.uniform(first_key, (D,), jnp.float32)
    column_scale = 0.3 * jnp.exp(math.log(3.0) * (position + jitter))
    random_part = jnp.clip(jax.random.normal(second_key, (N_GROUP, GROUP_TOKENS, D), jnp.float32), -4.0, 4.0)
    values = random_part * column_scale
    return values.astype(jnp.bfloat16)


def hidden_scale(key):
    position = jnp.arange(FF, dtype=jnp.float32) / FF
    jitter = jax.random.uniform(key, (FF,), jnp.float32)
    return jnp.exp(math.log(3.0) * (position - 0.5) + math.log(3.0) * (jitter - 0.5))


def random_matrix(key, shape):
    return jnp.clip(jax.random.normal(key, shape, jnp.float32), -4.0, 4.0)


def draw_w_in(key, part):
    first_key, second_key = jax.random.split(jax.random.fold_in(key, 11))
    column_scale = hidden_scale(first_key)
    return random_matrix(second_key, (D, FF)) * column_scale[None, :] / math.sqrt(D)


def draw_w_out(key, part):
    first_key, second_key = jax.random.split(jax.random.fold_in(key, 23))
    row_scale = hidden_scale(first_key)
    return random_matrix(second_key, (FF, D)) * row_scale[:, None] / math.sqrt(FF)


def steps_of(own_key, shape, shards, smallest, high):
    level = 1.0
    for dim, blocks in shards:
        draws = jax.random.uniform(jax.random.fold_in(jax.random.fold_in(own_key, 6), dim), (blocks,), jnp.float32, smallest / len(shards), high / len(shards))
        level = level * jnp.repeat(jnp.exp(draws), shape[dim] // blocks).reshape((-1,) + (1,) * (len(shape) - 1 - dim))
    return level


def bell_draw(stream_key, dims, deviation, limit, pieces=(), kind=jnp.bfloat16):
    array = jax.random.normal(stream_key, dims, jnp.float32) * deviation
    if len(pieces) > 0:
        array = steps_of(stream_key, dims, pieces, -0.22, 0.18) * array
    return jnp.clip(array, min=-limit, max=limit).astype(kind)


def setup_inputs(seed: int = 0) -> dict:
    splits = jax.random.split(jax.random.key(seed), 5)
    return {
        "inputs": draw_inputs(jax.random.fold_in(splits[4], 71), 0),
        "targets": bell_draw(splits[1], (N_GROUP, GROUP_TOKENS, D), 1.0, 4.0, ((1, 16), (2, 16))),
        "w_in": draw_w_in(jax.random.fold_in(splits[4], 71), 0),
        "w_out": draw_w_out(jax.random.fold_in(splits[4], 71), 0),
    }


root_half = 0.7071067811865476
inv_root_tau = 0.3989422804014327
radius_value = 1.0

def gelu_value(values):
    return 0.5 * values * (1.0 + lax.erf(values * root_half))

def gelu_slope(values):
    return 0.5 * (1.0 + lax.erf(values * root_half)) + values * jnp.exp(-0.5 * values * values) * inv_root_tau

def reference(inputs, targets, w_in, w_out):
    weights_in = w_in.astype(jnp.bfloat16)
    weights_out = w_out.astype(jnp.bfloat16)

    def group_step(sums, per_group):
        sum_in, sum_out = sums
        group_inputs, group_targets = per_group
        pre = jnp.dot(group_inputs, weights_in, preferred_element_type=jnp.float32)
        hidden = gelu_value(pre).astype(jnp.bfloat16)
        output = jnp.dot(hidden, weights_out, preferred_element_type=jnp.float32)
        errors = (output - group_targets.astype(jnp.float32)).astype(jnp.bfloat16)
        back = jnp.dot(errors, weights_out.T, preferred_element_type=jnp.float32)
        slopes = (back * gelu_slope(pre)).astype(jnp.bfloat16)
        ascent_in = jnp.dot(group_inputs.T, slopes, preferred_element_type=jnp.float32)
        ascent_out = jnp.dot(hidden.T, errors, preferred_element_type=jnp.float32)
        squares = jnp.sum(ascent_in * ascent_in) + jnp.sum(ascent_out * ascent_out)
        factor = radius_value * lax.rsqrt(squares + 1e-12)
        rounded_in = ascent_in.astype(jnp.bfloat16)
        rounded_out = ascent_out.astype(jnp.bfloat16)
        pre_two = pre + factor * jnp.dot(group_inputs, rounded_in, preferred_element_type=jnp.float32)
        hidden_two = gelu_value(pre_two).astype(jnp.bfloat16)
        output_two = jnp.dot(hidden_two, weights_out, preferred_element_type=jnp.float32) + factor * jnp.dot(hidden_two, rounded_out, preferred_element_type=jnp.float32)
        errors_two = (output_two - group_targets.astype(jnp.float32)).astype(jnp.bfloat16)
        back_two = jnp.dot(errors_two, weights_out.T, preferred_element_type=jnp.float32) + factor * jnp.dot(errors_two, rounded_out.T, preferred_element_type=jnp.float32)
        slopes_two = (back_two * gelu_slope(pre_two)).astype(jnp.bfloat16)
        sum_in = sum_in + jnp.dot(group_inputs.T, slopes_two, preferred_element_type=jnp.float32)
        sum_out = sum_out + jnp.dot(hidden_two.T, errors_two, preferred_element_type=jnp.float32)
        return ((sum_in, sum_out), factor)
    start_in = jnp.zeros(w_in.shape, jnp.float32)
    start_out = jnp.zeros(w_out.shape, jnp.float32)
    (sum_in, sum_out), unused = lax.scan(group_step, (start_in, start_out), (inputs, targets))
    groups = inputs.shape[0]
    return (sum_in / groups, sum_out / groups)
```

```python
import jax
import jax.numpy as jnp
from jax import lax
from jax.sharding import PartitionSpec as P

root_half = 0.7071067811865476
inv_root_tau = 0.3989422804014327
bf16 = jnp.bfloat16
f32 = jnp.float32


def gelu_value(values):
    return 0.5 * values * (1.0 + lax.erf(values * root_half))


def gelu_slope(values):
    return (
        0.5 * (1.0 + lax.erf(values * root_half))
        + values * jnp.exp(-0.5 * values * values) * inv_root_tau
    )


def swap_group(block, mask):
    return lax.ppermute(block, "group", [(k, k ^ mask) for k in range(16)])


def swap_ingroup(block, mask):
    return lax.ppermute(block, "ingroup", [(k, k ^ mask) for k in range(16)])


def swap_both(block, mask):
    return lax.ppermute(
        block, ("group", "ingroup"), [(k, k ^ (mask * 17)) for k in range(256)]
    )


def offset_of(block):
    return ((block & 3) << 2) | (((block >> 2) & 1) << 1) | (block >> 3)


starts = {mask: (mask & 1) * 128 + (mask >> 1) * 64 for mask in range(4)}


def scatter_group(partial):
    total = partial[0:64]
    for mask in (1, 3, 2):
        block = partial[starts[mask] : starts[mask] + 64].astype(bf16)
        total = total + swap_group(block, mask).astype(f32)
    own = total[0:16]
    for mask in (1, 2, 3):
        block = total[16 * mask : 16 * mask + 16].astype(bf16)
        own = own + swap_group(block, 4 * mask).astype(f32)
    return own


def gather_group(own):
    quarter = jnp.concatenate([own] + [swap_group(own, 4 * mask) for mask in (1, 2, 3)], axis=0)
    others = {mask: swap_group(quarter, mask) for mask in (1, 3, 2)}
    return jnp.concatenate([quarter, others[2], others[1], others[3]], axis=0)


def scatter_ingroup(partial):
    half = partial[0:128] + swap_ingroup(partial[128:256], 1)
    pair = jnp.concatenate([half[0:16], half[64:80]], axis=0)
    for mask in (1, 3, 2):
        block = jnp.concatenate(
            [half[16 * mask : 16 * mask + 16], half[64 + 16 * mask : 80 + 16 * mask]], axis=0
        )
        pair = pair + swap_ingroup(block, 4 * mask)
    other = swap_ingroup(pair, 2)
    return pair + jnp.concatenate([other[16:32], other[0:16]], axis=0)


def gather_ingroup(pair):
    others = {mask: swap_ingroup(pair, 4 * mask) for mask in (1, 3, 2)}
    parts = [pair, others[1], others[2], others[3]]
    half = jnp.concatenate([v[0:16] for v in parts] + [v[16:32] for v in parts], axis=0)
    return jnp.concatenate([half, swap_ingroup(half, 1)], axis=0)


def gather_tokens(own):
    value = jnp.concatenate([own, swap_ingroup(own, 2)], axis=0)
    others = {mask: swap_ingroup(value, 4 * mask) for mask in (1, 3, 2)}
    value = jnp.concatenate([value, others[1], others[2], others[3]], axis=0)
    return jnp.concatenate([value, swap_ingroup(value, 1)], axis=0)


def sum_own_group(value):
    value = value + swap_both(value, 1)
    value = value + swap_both(value, 2)
    return value + swap_both(value, 4) + swap_both(value, 8) + swap_both(value, 12)


def dot(a, b):
    return lax.dot_general(a, b, (((1,), (0,)), ((), ())), preferred_element_type=f32)


def dot_rows(a, b):
    return lax.dot_general(a, b, (((0,), (0,)), ((), ())), preferred_element_type=f32)


def dot_cols(a, b):
    return lax.dot_general(a, b, (((1,), (1,)), ((), ())), preferred_element_type=f32)


def dot_small(a, b):
    return lax.dot_general(
        a, b, (((1,), (0,)), ((), ())), precision=lax.Precision.HIGHEST,
        preferred_element_type=f32,
    )


def per_device(inputs, targets, w_in, w_out):
    weights_in = w_in.astype(bf16)
    weights_out = w_out.astype(bf16)
    wide = w_in.shape[1]
    groups = 16
    me_group = lax.axis_index("group")
    me_in = lax.axis_index("ingroup")

    row = lax.broadcasted_iota(jnp.int32, (256, 256), 0)
    col = lax.broadcasted_iota(jnp.int32, (256, 256), 1)
    slot = col >> 4
    slot = (((slot >> 1) & 3) << 2) | ((slot & 1) << 1) | (slot >> 3)
    pick = ((slot ^ me_in) == (row & 15)) & (
        (col & 15) == (offset_of(row >> 4) ^ me_group ^ me_in)
    )
    pick = pick.astype(bf16)
    same = (row >> 4) == (col >> 4)
    fold = ((col[:, 0:128] == (row[:, 0:128] & 15))).astype(f32)

    features = dot(pick, gather_tokens(inputs[:, 0, :])).astype(bf16)
    wanted = dot(
        jnp.concatenate([pick[0:16], pick[64:80]], axis=0), gather_tokens(targets[:, 0, :])
    )

    def small_gram(rows):
        gram = jnp.where(same, dot_cols(rows, rows), 0.0)
        gram = gram.reshape(256, 2, 128)
        gram = gram[:, 0] + gram[:, 1]
        for shift in (64, 32, 16):
            gram = gram + jnp.roll(gram, shift, axis=1)
        return gram

    def residuals(partial_out):
        pair = (scatter_ingroup(partial_out) - wanted).astype(bf16)
        return gather_ingroup(pair)

    pre_ext = scatter_group(
        jnp.concatenate([dot(features, weights_in), small_gram(features)], axis=1)
    )
    pre = pre_ext[:, 0:wide]
    gram_in = pre_ext[:, wide : wide + 16]
    hidden_own = gelu_value(pre).astype(bf16)
    hidden = gather_group(hidden_own)
    errors = residuals(dot(hidden, weights_out))
    back_ext = scatter_group(
        jnp.concatenate([dot_cols(errors, weights_out), small_gram(errors)], axis=1)
    )
    gram_errors = back_ext[:, wide : wide + 16]
    slopes_own = (back_ext[:, 0:wide] * gelu_slope(pre)).astype(bf16)

    slopes_f = slopes_own.astype(f32)
    hidden_f = hidden_own.astype(f32)
    shift = dot_small(gram_in, slopes_f)
    squares = jnp.sum(shift * slopes_f + dot_small(gram_errors, hidden_f) * hidden_f)
    squares = sum_own_group(jnp.full((8, 128), squares))
    radius = lax.rsqrt(squares + 1e-12)[0:1, 0:1]
    pre_two = pre + radius * shift
    hidden_two_own = gelu_value(pre_two).astype(bf16)
    radius_high = radius.astype(bf16)
    radius_low = (radius - radius_high.astype(f32)).astype(bf16)
    lane = lax.broadcasted_iota(jnp.int32, (16, 128), 1)
    tail = jnp.where(lane == 0, radius_high, radius_low)
    two_ext = gather_group(jnp.concatenate([hidden_two_own, tail], axis=1))
    hidden_two = two_ext[:, 0:wide]
    radii = two_ext[:, wide : wide + 1].astype(f32) + two_ext[:, wide + 1 : wide + 2].astype(f32)

    scaled = jnp.where(same, radii, 0.0)
    mix_hidden = (scaled * dot_cols(hidden_two, hidden)).astype(bf16)
    errors_two = residuals(dot(hidden_two, weights_out) + dot(mix_hidden, errors))
    mix_errors = (scaled * dot_cols(errors_two, errors)).astype(bf16)
    back_two = scatter_group(dot_cols(errors_two, weights_out) + dot(mix_errors, hidden))
    slopes_two = gather_group((back_two * gelu_slope(pre_two)).astype(bf16))
    grad_out = dot_rows(hidden_two, errors_two)
    grad_in = dot_rows(features, slopes_two)
    return (grad_in / groups, grad_out / groups)


def solution(mesh):
    return jax.shard_map(
        per_device,
        mesh=mesh,
        in_specs=(
            P(None, "ingroup", "group"),
            P(None, "ingroup", "group"),
            P("group", "ingroup"),
            P("ingroup", "group"),
        ),
        out_specs=(P("group", "ingroup"), P("ingroup", "group")),
        check_vma=False,
    )
```

```python
import jax
import jax.numpy as jnp
from jax import lax
from jax.sharding import PartitionSpec as P

root_half = 0.7071067811865476
inv_root_tau = 0.3989422804014327
bf16 = jnp.bfloat16
f32 = jnp.float32


def gelu_value(values):
    return 0.5 * values * (1.0 + lax.erf(values * root_half))


def gelu_slope(values):
    return (
        0.5 * (1.0 + lax.erf(values * root_half))
        + values * jnp.exp(-0.5 * values * values) * inv_root_tau
    )


def flip(index):
    return (index & 12) | ((index & 1) << 1) | ((index >> 1) & 1)


def swap_group(block, mask):
    return lax.ppermute(block, "group", [(k, k ^ mask) for k in range(16)])


def swap_ingroup(block, offset):
    return lax.ppermute(block, "ingroup", [(k, k ^ flip(offset)) for k in range(16)])


def swap_both(block, mask):
    step = flip(mask) * 16 + mask
    return lax.ppermute(block, ("group", "ingroup"), [(k, k ^ step) for k in range(256)])


def block(piece, a):
    return piece[16 * a : 16 * a + 16]


def scatter_group(pieces, dtype):
    moved = {b: swap_group(pieces[b].astype(dtype), b) for b in (2, 1, 3)}
    total = pieces[0]
    for b in (1, 3, 2):
        total = total + moved[b].astype(f32)
    moved = {a: swap_group(block(total, a).astype(dtype), 4 * a) for a in (3, 2, 1)}
    own = block(total, 0)
    for a in (1, 2, 3):
        own = own + moved[a].astype(f32)
    return own


def gather_group(own):
    moved = {a: swap_group(own, 4 * a) for a in (3, 2, 1)}
    quarter = jnp.concatenate([own, moved[1], moved[2], moved[3]], axis=0)
    moved = {b: swap_group(quarter, b) for b in (2, 1, 3)}
    return [quarter, moved[1], moved[2], moved[3]]


def sum_ingroup(pieces):
    moved = {b: swap_ingroup(pieces[b].astype(bf16), b) for b in (1, 3, 2)}
    total = pieces[0]
    for b in (1, 3, 2):
        total = total + moved[b].astype(f32)
    sent = total.astype(bf16)
    moved = {a: swap_ingroup(sent, 4 * a) for a in (2, 1, 3)}
    blocks = []
    for k in range(4):
        value = block(total, k)
        for a in (1, 2, 3):
            value = value + block(moved[a], k ^ a).astype(f32)
        blocks.append(value)
    return jnp.concatenate(blocks, axis=0)


def gather_ingroup(piece):
    moved = {b: swap_ingroup(piece, b) for b in (1, 3, 2)}
    return [piece, moved[1], moved[2], moved[3]]


def sum_own_group(value):
    value = value + swap_both(value, 8) + swap_both(value, 12) + swap_both(value, 4)
    return value + swap_both(value, 2) + swap_both(value, 3) + swap_both(value, 1)


def dot(a, b):
    return lax.dot_general(a, b, (((1,), (0,)), ((), ())), preferred_element_type=f32)


def dot_rows(a, b):
    return lax.dot_general(a, b, (((0,), (0,)), ((), ())), preferred_element_type=f32)


def dot_cols(a, b):
    return lax.dot_general(a, b, (((1,), (1,)), ((), ())), preferred_element_type=f32)


def dot_small(a, b):
    return lax.dot_general(
        a, b, (((1,), (0,)), ((), ())), precision=lax.Precision.HIGHEST,
        preferred_element_type=f32,
    )


def iota(shape, dim):
    return lax.broadcasted_iota(jnp.int32, shape, dim)


def per_device(inputs, targets, w_in, w_out):
    weights_in = w_in.astype(bf16)
    weights_out = w_out.astype(bf16)
    wide = w_in.shape[1]
    groups = 16
    me_in = lax.axis_index("ingroup")
    me = lax.axis_index("group") ^ flip(me_in)

    own = inputs[:, 0, :]
    quad = {m: lax.ppermute(own, "ingroup", [(k, k ^ m) for k in range(16)]) for m in (2, 3, 1)}
    quad = jnp.concatenate([own, quad[1], quad[2], quad[3]], axis=0)
    every = {c: lax.ppermute(quad, "ingroup", [(k, k ^ (4 * c)) for k in range(16)]) for c in (2, 1, 3)}
    every = jnp.concatenate([quad, every[1], every[2], every[3]], axis=0)

    row, col = iota((64, 256), 0), iota((64, 256), 1)
    token_of = (col >> 4) ^ me_in
    features = []
    for b in range(4):
        pick = (token_of == (row & 15)) & ((col & 15) == (((row >> 4) << 2 | b) ^ me))
        features.append(dot(pick.astype(bf16), every).astype(bf16))

    row, col = iota((64, 64), 0), iota((64, 64), 1)
    same = (row >> 4) == (col >> 4)
    row, col = iota((64, 32), 0), iota((64, 32), 1)
    fold_in = ((row & 15) == col).astype(f32)
    fold_out = (((row & 15) + 16) == col).astype(f32)

    def gram(rows):
        return jnp.where(same, dot_cols(rows, rows), 0.0)

    pre = scatter_group([dot(v, weights_in) for v in features], bf16)
    hidden_own = gelu_value(pre).astype(bf16)
    hidden = gather_group(hidden_own)
    row, col = iota((16, 16), 0), iota((16, 16), 1)
    pick = col == (((row & 3) << 2 | (row >> 2)) ^ me)
    late = lax.optimization_barrier((targets, hidden[0]))[0]
    own = dot(pick.astype(bf16), late[:, 0, :]).astype(bf16)
    quad = [own[0:4]]
    for m in (1, 2, 3):
        b = flip(m)
        part = own[4 * b : 4 * b + 4]
        quad.append(lax.ppermute(part, "ingroup", [(k, k ^ m) for k in range(16)]))
    quad = jnp.concatenate(quad, axis=0)
    rest = [lax.ppermute(quad, "ingroup", [(k, k ^ (4 * c)) for k in range(16)]) for c in (1, 2, 3)]
    row, col = iota((64, 64), 0), iota((64, 64), 1)
    pick = (((col >> 2) ^ me_in) == (row & 15)) & (((col & 3) ^ (col >> 4)) == (row >> 4))
    wanted = dot(pick.astype(bf16), jnp.concatenate([quad] + rest, axis=0))

    def residuals(parts):
        return gather_ingroup((sum_ingroup(parts) - wanted).astype(bf16))

    errors = residuals([dot(v, weights_out) for v in hidden])
    back = scatter_group([dot_cols(v, weights_out) for v in errors], bf16)
    grams = scatter_group(
        [
            dot_small(gram(v), fold_in) + dot_small(gram(w), fold_out)
            for v, w in zip(features, errors)
        ],
        f32,
    )
    slopes_f = (back * gelu_slope(pre)).astype(bf16).astype(f32)
    hidden_f = hidden_own.astype(f32)
    shift = dot_small(grams[:, 0:16], slopes_f)
    squares = jnp.sum(shift * slopes_f + dot_small(grams[:, 16:32], hidden_f) * hidden_f)
    squares = sum_own_group(jnp.full((8, 128), squares))
    radius = lax.rsqrt(squares + 1e-12)[0:1, 0:1]
    pre_two = pre + radius * shift
    hidden_two_own = gelu_value(pre_two).astype(bf16)
    radius_high = radius.astype(bf16)
    radius_low = (radius - radius_high.astype(f32)).astype(bf16)
    tail = jnp.where(iota((16, 128), 1) == 0, radius_high, radius_low)
    both = gather_group(jnp.concatenate([hidden_two_own, tail], axis=1))
    hidden_two = [v[:, 0:wide] for v in both]
    scaled = [
        jnp.where(same, v[:, wide : wide + 1].astype(f32) + v[:, wide + 1 : wide + 2].astype(f32), 0.0)
        for v in both
    ]

    errors_two = residuals(
        [
            dot(h2, weights_out) + dot((s * dot_cols(h2, h)).astype(bf16), e)
            for h2, s, h, e in zip(hidden_two, scaled, hidden, errors)
        ]
    )
    back_two = scatter_group(
        [
            dot_cols(e2, weights_out) + dot((s * dot_cols(e2, e)).astype(bf16), h)
            for e2, s, h, e in zip(errors_two, scaled, hidden, errors)
        ],
        bf16,
    )
    slopes_two = gather_group((back_two * gelu_slope(pre_two)).astype(bf16))
    grad_out = sum(dot_rows(hidden_two[b], errors_two[b]) for b in (0, 1, 3, 2))
    grad_in = sum(dot_rows(features[b], slopes_two[b]) for b in (0, 1, 3, 2))
    return (grad_in / groups, grad_out / groups)


def solution(mesh):
    return jax.shard_map(
        per_device,
        mesh=mesh,
        in_specs=(
            P(None, "ingroup", "group"),
            P(None, "ingroup", "group"),
            P("group", "ingroup"),
            P("ingroup", "group"),
        ),
        out_specs=(P("group", "ingroup"), P("ingroup", "group")),
        check_vma=False,
    )
```

```python
import jax
import jax.numpy as jnp
from jax import lax
from jax.sharding import Mesh, PartitionSpec as P

root_half = 0.7071067811865476
inv_root_tau = 0.3989422804014327
bf16 = jnp.bfloat16
f32 = jnp.float32


def gelu_value(values):
    return 0.5 * values * (1.0 + lax.erf(values * root_half))


def gelu_slope(values):
    return (
        0.5 * (1.0 + lax.erf(values * root_half))
        + values * jnp.exp(-0.5 * values * values) * inv_root_tau
    )


def swap(value, axis):
    return lax.ppermute(value, axis, [(0, 1), (1, 0)])


def swap_x(value, b, k):
    pairs = [(n, n ^ (2 * b + k)) for n in range(4)]
    return lax.ppermute(value, ("xh", "xl"), pairs)


def exchange(value, axis):
    return lax.all_to_all(value, axis, 0, 0, tiled=False)


def scatter_group(pieces):
    total = pieces[0, 0]
    moved = [swap_x(pieces[b, k].astype(bf16), b, k) for b, k in ((1, 0), (0, 1), (1, 1))]
    total = total + moved[1].astype(f32) + moved[2].astype(f32) + moved[0].astype(f32)
    parts = exchange(total.astype(bf16).reshape(4, 16, total.shape[1]), "zl")
    return jnp.sum(parts.astype(f32), axis=0)


def gather_group(own):
    wide = own.shape[1]
    piece = exchange(jnp.broadcast_to(own[None], (4, 16, wide)), "zl").reshape(64, wide)
    moved = {(b, k): swap_x(piece, b, k) for b, k in ((1, 0), (0, 1), (1, 1))}
    moved[0, 0] = piece
    return moved


def dot(a, b):
    return lax.dot_general(a, b, (((1,), (0,)), ((), ())), preferred_element_type=f32)


def dot_rows(a, b):
    return lax.dot_general(a, b, (((0,), (0,)), ((), ())), preferred_element_type=f32)


def dot_cols(a, b):
    return lax.dot_general(a, b, (((1,), (1,)), ((), ())), preferred_element_type=f32)


def dot_small(a, b):
    return lax.dot_general(
        a, b, (((1,), (0,)), ((), ())), precision=lax.Precision.HIGHEST,
        preferred_element_type=f32,
    )


def iota(shape, dim):
    return lax.broadcasted_iota(jnp.int32, shape, dim)


def per_device(inputs, targets, w_in, w_out):
    wide = w_in.shape[1]
    width = w_in.shape[0]
    groups = 16
    zh, core = lax.axis_index("zh"), lax.axis_index("c")
    xh, xl = lax.axis_index("xh"), lax.axis_index("xl")
    keep = xl == 0

    def in_order(own, other):
        return jnp.where(keep, own, other), jnp.where(keep, other, own)

    both = jnp.concatenate([inputs[:, 0, :], targets[:, 0, :]], axis=0).reshape(16, 2, width)
    mine = jnp.where(core == 0, both[:, 0], both[:, 1])
    theirs = jnp.where(core == 0, both[:, 1], both[:, 0])
    theirs = swap(theirs, "c")
    pair = jnp.concatenate([mine[0:8], theirs[0:8], mine[8:16], theirs[8:16]], axis=0)
    other = swap(pair, "zh")
    wanted = jnp.concatenate([pair[16:32], other[16:32]], axis=0).astype(f32)
    every = jnp.concatenate([pair[0:16], other[0:16]], axis=0)
    every = exchange(jnp.broadcast_to(every[None], (4, 32, width)), "y").reshape(128, width)

    w_in_b = w_in.astype(bf16)
    w_out_b = w_out.astype(bf16)
    weights_in = in_order(w_in_b, swap(w_in_b, "c"))
    weights_out = in_order(w_out_b, swap(w_out_b, "c"))

    row, col = iota((128, 128), 0), iota((128, 128), 1)
    token = ((col >> 5) << 2) | ((((col >> 4) & 1) ^ zh) << 1) | (((col >> 3) & 1) ^ core)
    group = ((row >> 4) & 3) << 1 | ((row >> 6) ^ xh)
    pick = ((token == (row & 15)) & ((col & 7) == group)).astype(bf16)

    row, col = iota((64, 64), 0), iota((64, 64), 1)
    same = (row >> 4) == (col >> 4)
    row, col = iota((64, 128), 0), iota((64, 128), 1)
    fold = ((row & 15) == col).astype(bf16)

    def with_gram(product, gram):
        lanes = dot(jnp.where(same, gram, 0.0).astype(bf16), fold)
        return jnp.concatenate([product, lanes], axis=1)

    def residuals(parts):
        rows = dot_rows(pick, jnp.concatenate([v.astype(bf16) for v in parts], axis=0))
        moved = exchange(rows.astype(bf16).reshape(4, 32, width), "y")
        total = jnp.sum(moved.astype(f32), axis=0)
        other = swap(total, "zh")
        total = total + jnp.concatenate([other[16:32], other[0:16]], axis=0)
        own = (total - wanted).astype(bf16)
        every = exchange(jnp.broadcast_to(own[None], (4, 32, width)), "y").reshape(128, width)
        rows = dot(pick, every).astype(bf16)
        return rows[0:64], rows[64:128]

    order = ((1, 0), (0, 1), (1, 1), (0, 0))
    features = dot(pick, every).astype(bf16)
    features = features[0:64], features[64:128]
    grams = [dot_cols(v, v) for v in features]
    pre_ext = scatter_group(
        {(b, k): with_gram(dot(features[b], weights_in[k]), grams[b]) for b, k in order}
    )
    pre, gram_in = pre_ext[:, 0:wide], pre_ext[:, wide : wide + 16]
    hidden_own = gelu_value(pre).astype(bf16)
    hidden = gather_group(hidden_own)
    errors = residuals(
        [dot(hidden[b, 0], weights_out[0]) + dot(hidden[b, 1], weights_out[1]) for b in (0, 1)]
    )
    grams = [dot_cols(v, v) for v in errors]
    back_ext = scatter_group(
        {(b, k): with_gram(dot_cols(errors[b], weights_out[k]), grams[b]) for b, k in order}
    )
    back, gram_errors = back_ext[:, 0:wide], back_ext[:, wide : wide + 16]
    slopes_f = (back * gelu_slope(pre)).astype(bf16).astype(f32)
    hidden_f = hidden_own.astype(f32)
    shift = dot_small(gram_in, slopes_f)
    squares = jnp.sum(shift * slopes_f + dot_small(gram_errors, hidden_f) * hidden_f)
    squares = exchange(jnp.full((16, 8, 128), squares), ("xl", "y", "zh"))
    squares = jnp.sum(squares, axis=0)
    radius = lax.rsqrt(squares + 1e-12)[0:1, 0:1]
    pre_two = pre + radius * shift
    hidden_two_own = gelu_value(pre_two).astype(bf16)
    radius_high = radius.astype(bf16)
    radius_low = (radius - radius_high.astype(f32)).astype(bf16)
    tail = jnp.where(iota((16, 128), 1) == 0, radius_high, radius_low)
    two = gather_group(jnp.concatenate([hidden_two_own, tail], axis=1))
    hidden_two = {at: v[:, 0:wide] for at, v in two.items()}
    scaled = [
        jnp.where(
            same,
            two[b, 0][:, wide : wide + 1].astype(f32) + two[b, 0][:, wide + 1 : wide + 2].astype(f32),
            0.0,
        )
        for b in (0, 1)
    ]
    mixed = [
        scaled[b] * (dot_cols(hidden_two[b, 0], hidden[b, 0]) + dot_cols(hidden_two[b, 1], hidden[b, 1]))
        for b in (0, 1)
    ]
    errors_two = residuals(
        [
            dot(hidden_two[b, 0], weights_out[0])
            + dot(hidden_two[b, 1], weights_out[1])
            + dot(mixed[b].astype(bf16), errors[b])
            for b in (0, 1)
        ]
    )
    mixed = [(scaled[b] * dot_cols(errors_two[b], errors[b])).astype(bf16) for b in (0, 1)]
    back_two = scatter_group(
        {
            (b, k): dot_cols(errors_two[b], weights_out[k]) + dot(mixed[b], hidden[b, k])
            for b, k in order
        }
    )
    slopes_two = gather_group((back_two * gelu_slope(pre_two)).astype(bf16))

    def rows_of(parts):
        first, second = (jnp.concatenate([parts[0, k], parts[1, k]], axis=0) for k in (0, 1))
        return in_order(first, second)

    features = jnp.concatenate(features, axis=0)
    errors_two = jnp.concatenate(errors_two, axis=0)
    own, other = rows_of(hidden_two)
    other = swap(dot_rows(other, errors_two).astype(bf16), "c")
    grad_out = (dot_rows(own, errors_two) + other.astype(f32)) / groups
    own, other = rows_of(slopes_two)
    other = swap(dot_rows(features, other).astype(bf16), "c")
    grad_in = (dot_rows(features, own) + other.astype(f32)) / groups
    return grad_in, grad_out


def solution(mesh):
    fine = Mesh(mesh.devices.reshape(4, 2, 2, 4, 2, 2), ("zl", "xh", "xl", "y", "zh", "c"))
    group, ingroup = ("zl", "xh", "xl"), ("y", "zh", "c")
    return jax.shard_map(
        per_device,
        mesh=fine,
        in_specs=(
            P(None, ingroup, group),
            P(None, ingroup, group),
            P(group, ingroup),
            P(ingroup, group),
        ),
        out_specs=(P(group, ingroup), P(ingroup, group)),
        check_vma=False,
    )
```

```python
import jax
import jax.numpy as jnp
from jax import lax
from jax.sharding import Mesh, PartitionSpec as P

root_half = 0.7071067811865476
inv_root_tau = 0.3989422804014327
bf16 = jnp.bfloat16
f32 = jnp.float32


def gelu_value(values):
    return 0.5 * values * (1.0 + lax.erf(values * root_half))


def gelu_slope(values):
    return (
        0.5 * (1.0 + lax.erf(values * root_half))
        + values * jnp.exp(-0.5 * values * values) * inv_root_tau
    )


def swap(value, axis):
    return lax.ppermute(value, axis, [(0, 1), (1, 0)])


def swap_x(value, b, k):
    pairs = [(n, n ^ (4 * b + 3 * k)) for n in range(8)]
    return lax.ppermute(value, ("xh", "xl", "c"), pairs)


def swap_z(value, a):
    return lax.ppermute(value, "zl", [(n, n ^ a) for n in range(4)])


def exchange(value, axis):
    return lax.all_to_all(value, axis, 0, 0, tiled=False)


def scatter_x(pieces):
    moved = [swap_x(pieces[b, k].astype(bf16), b, k) for b, k in ((1, 0), (0, 1), (1, 1))]
    return pieces[0, 0] + moved[1].astype(f32) + moved[2].astype(f32) + moved[0].astype(f32)


def scatter_z(total):
    own = total[0:16]
    moved = {a: swap_z(total[16 * a : 16 * a + 16].astype(bf16), a) for a in (3, 2, 1)}
    return own + moved[1].astype(f32) + moved[2].astype(f32) + moved[3].astype(f32)


def gather_z(own):
    return [own] + [swap_z(own, a) for a in (1, 2, 3)]


def gather_x(piece):
    moved = {(b, k): swap_x(piece, b, k) for b, k in ((1, 0), (0, 1), (1, 1))}
    moved[0, 0] = piece
    return moved


def gather_group(own):
    return gather_x(jnp.concatenate(gather_z(own), axis=0))


def dot(a, b):
    return lax.dot_general(a, b, (((1,), (0,)), ((), ())), preferred_element_type=f32)


def dot_rows(a, b):
    return lax.dot_general(a, b, (((0,), (0,)), ((), ())), preferred_element_type=f32)


def dot_cols(a, b):
    return lax.dot_general(a, b, (((1,), (1,)), ((), ())), preferred_element_type=f32)


def dot_small(a, b):
    return lax.dot_general(
        a, b, (((1,), (0,)), ((), ())), precision=lax.Precision.HIGHEST,
        preferred_element_type=f32,
    )


def iota(shape, dim):
    return lax.broadcasted_iota(jnp.int32, shape, dim)


def per_device(inputs, targets, w_in, w_out):
    wide = w_in.shape[1]
    width = w_in.shape[0]
    groups = 16
    zh, core = lax.axis_index("zh"), lax.axis_index("c")
    xh, zl = lax.axis_index("xh"), lax.axis_index("zl")
    third = core ^ lax.axis_index("xl")

    both = jnp.concatenate([inputs[:, 0, :], targets[:, 0, :]], axis=0).reshape(16, 2, width)
    mine = jnp.where(third == 0, both[:, 0], both[:, 1])
    theirs = jnp.where(third == 0, both[:, 1], both[:, 0])
    theirs = swap(theirs, "c")
    pair = jnp.concatenate([mine[0:8], theirs[0:8], mine[8:16], theirs[8:16]], axis=0)
    other = swap(pair, "zh")
    wanted = jnp.concatenate([pair[16:32], other[16:32]], axis=0).astype(f32)
    every = jnp.concatenate([pair[0:16], other[0:16]], axis=0)

    w_in_b = w_in.astype(bf16)
    w_out_b = w_out.astype(bf16)
    every, w_in_b, w_out_b = lax.optimization_barrier((every, w_in_b, w_out_b))
    weights_in = w_in_b, swap(w_in_b, "c")
    weights_out = w_out_b, swap(w_out_b, "c")
    every = exchange(jnp.broadcast_to(every[None], (4, 32, width)), "y").reshape(128, width)

    row, col = iota((128, 128), 0), iota((128, 128), 1)
    token = ((col >> 5) << 2) | ((((col >> 4) & 1) ^ zh) << 1) | (((col >> 3) & 1) ^ core)
    group = (((row >> 4) & 3) ^ zl) << 1 | ((row >> 6) ^ xh)
    pick = ((token == (row & 15)) & ((col & 7) == group)).astype(bf16)

    row, col = iota((64, 64), 0), iota((64, 64), 1)
    same = (row >> 4) == (col >> 4)
    row, col = iota((64, 128), 0), iota((64, 128), 1)
    fold = ((row & 15) == col).astype(bf16)

    def with_gram(product, gram):
        lanes = dot(jnp.where(same, gram, 0.0).astype(bf16), fold)
        return jnp.concatenate([product, lanes], axis=1)

    def residuals(parts):
        rows = dot_rows(pick, jnp.concatenate([v.astype(bf16) for v in parts], axis=0))
        moved = exchange(rows.astype(bf16).reshape(4, 32, width), "y")
        total = jnp.sum(moved.astype(f32), axis=0)
        other = swap(total, "zh")
        total = total + jnp.concatenate([other[16:32], other[0:16]], axis=0)
        own = (total - wanted).astype(bf16)
        every = exchange(jnp.broadcast_to(own[None], (4, 32, width)), "y").reshape(128, width)
        rows = dot(pick, every).astype(bf16)
        return rows[0:64], rows[64:128]

    order = ((1, 0), (0, 1), (1, 1), (0, 0))
    features_all = dot(pick, every).astype(bf16)
    features = features_all[0:64], features_all[64:128]
    grams = [dot_cols(v, v) for v in features]
    total = scatter_x(
        {(b, k): with_gram(dot(features[b], weights_in[k]), grams[b]) for b, k in order}
    )
    low = (zl & 1) == 0
    parts = total.astype(bf16).reshape(2, 2, 16, total.shape[1])
    parts = jnp.where(low, parts, parts[:, ::-1])
    parts = jnp.where(zl < 2, parts, parts[::-1]).reshape(4, 16, total.shape[1])
    pre_ext = jnp.sum(exchange(parts, "zl").astype(f32), axis=0)
    pre, gram_in = pre_ext[:, 0:wide], pre_ext[:, wide : wide + 16]
    hidden_own = gelu_value(pre).astype(bf16)
    hidden = gather_group(hidden_own)
    errors = residuals(
        [dot(hidden[b, 0], weights_out[0]) + dot(hidden[b, 1], weights_out[1]) for b in (0, 1)]
    )
    grams = [dot_cols(v, v) for v in errors]
    total = scatter_x(
        {(b, k): with_gram(dot_cols(errors[b], weights_out[k]), grams[b]) for b, k in order}
    )
    back_ext = scatter_z(total)
    back, gram_errors = back_ext[:, 0:wide], back_ext[:, wide : wide + 16]
    slopes_f = (back * gelu_slope(pre)).astype(bf16).astype(f32)
    hidden_f = hidden_own.astype(f32)
    shift = dot_small(gram_in, slopes_f)
    squares = jnp.sum(shift * slopes_f + dot_small(gram_errors, hidden_f) * hidden_f)
    squares = jnp.sum(exchange(jnp.full((8, 8, 128), squares), ("y", "zh")), axis=0)
    squares = squares + swap_x(squares, 0, 1)
    radius = lax.rsqrt(squares + 1e-12)[0:1, 0:1]
    pre_two = pre + radius * shift
    hidden_two_own = gelu_value(pre_two).astype(bf16)
    radius_high = radius.astype(bf16)
    radius_low = (radius - radius_high.astype(f32)).astype(bf16)
    tail = jnp.where(iota((16, 128), 1) == 0, radius_high, radius_low)
    two = gather_z(jnp.concatenate([hidden_two_own, tail], axis=1))
    lanes = jnp.concatenate([v[:, wide:] for v in two], axis=0)
    hidden_two = gather_x(jnp.concatenate([v[:, 0:wide] for v in two], axis=0))
    scaled = [
        jnp.where(same, v[:, 0:1].astype(f32) + v[:, 1:2].astype(f32), 0.0)
        for v in (lanes, swap_x(lanes, 1, 0))
    ]
    mixed = [
        scaled[b] * (dot_cols(hidden_two[b, 0], hidden[b, 0]) + dot_cols(hidden_two[b, 1], hidden[b, 1]))
        for b in (0, 1)
    ]
    errors_two = residuals(
        [
            dot(hidden_two[b, 0], weights_out[0])
            + dot(hidden_two[b, 1], weights_out[1])
            + dot(mixed[b].astype(bf16), errors[b])
            for b in (0, 1)
        ]
    )
    mixed = [(scaled[b] * dot_cols(errors_two[b], errors[b])).astype(bf16) for b in (0, 1)]
    pieces = {
        (b, k): (dot_cols(errors_two[b], weights_out[k]) + dot(mixed[b], hidden[b, k])).astype(
            f32 if (b, k) == (0, 0) else bf16
        )
        for b, k in order
    }
    total = scatter_x(pieces)
    errors_all = jnp.concatenate(errors_two, axis=0)
    errors_all = lax.optimization_barrier((total, errors_all))[1]

    def rows_of(parts, k):
        return jnp.concatenate([parts[0, k], parts[1, k]], axis=0)

    other = swap(dot_rows(rows_of(hidden_two, 1), errors_all).astype(bf16), "c")
    back_two = scatter_z(total)
    slopes_two = (back_two * gelu_slope(pre_two)).astype(bf16)
    slopes_two, grad_out = lax.optimization_barrier((slopes_two, other))
    slopes_two = gather_group(slopes_two)
    slopes_two = lax.optimization_barrier(slopes_two)

    grad_out = (dot_rows(rows_of(hidden_two, 0), errors_all) + grad_out.astype(f32)) / groups
    other = swap(dot_rows(features_all, rows_of(slopes_two, 1)).astype(bf16), "c")
    grad_in = (dot_rows(features_all, rows_of(slopes_two, 0)) + other.astype(f32)) / groups
    return grad_in, grad_out


def solution(mesh):
    fine = Mesh(mesh.devices.reshape(4, 2, 2, 4, 2, 2), ("zl", "xh", "xl", "y", "zh", "c"))
    group, ingroup = ("zl", "xh", "xl"), ("y", "zh", "c")
    return jax.shard_map(
        per_device,
        mesh=fine,
        in_specs=(
            P(None, ingroup, group),
            P(None, ingroup, group),
            P(group, ingroup),
            P(ingroup, group),
        ),
        out_specs=(P(group, ingroup), P(ingroup, group)),
        check_vma=False,
    )
```

```python
import jax
import jax.numpy as jnp
from jax import lax
from jax.experimental import pallas as pl
from jax.experimental.pallas import tpu as pltpu
from jax.sharding import Mesh, PartitionSpec as P

root_half = 0.7071067811865476
inv_root_tau = 0.3989422804014327
bf16 = jnp.bfloat16
f32 = jnp.float32


def gelu_value(values):
    return 0.5 * values * (1.0 + lax.erf(values * root_half))


def gelu_slope(values):
    return (
        0.5 * (1.0 + lax.erf(values * root_half))
        + values * jnp.exp(-0.5 * values * values) * inv_root_tau
    )


def swap(value, axis):
    return lax.ppermute(value, axis, [(0, 1), (1, 0)])


def swap_x(value, b, k):
    pairs = [(n, n ^ (2 * b + k)) for n in range(4)]
    return lax.ppermute(value, ("xh", "xl"), pairs)


def exchange(value, axis):
    return lax.all_to_all(value, axis, 0, 0, tiled=False)


def swap_z(value, a):
    return lax.ppermute(value, "zl", [(n, n ^ a) for n in range(4)])


def scatter_x(pieces):
    moved = [swap_x(pieces[b, k].astype(bf16), b, k) for b, k in ((1, 0), (0, 1), (1, 1))]
    return pieces[0, 0] + moved[1].astype(f32) + moved[2].astype(f32) + moved[0].astype(f32)


def scatter_z(total):
    own = total[0:16]
    moved = {a: swap_z(total[16 * a : 16 * a + 16].astype(bf16), a) for a in (3, 2, 1)}
    return own + moved[1].astype(f32) + moved[2].astype(f32) + moved[3].astype(f32)


def gather_group(own):
    piece = jnp.concatenate([own] + [swap_z(own, a) for a in (1, 2, 3)], axis=0)
    moved = {(b, k): swap_x(piece, b, k) for b, k in ((1, 0), (0, 1), (1, 1))}
    moved[0, 0] = piece
    return moved


def dot(a, b):
    return lax.dot_general(a, b, (((1,), (0,)), ((), ())), preferred_element_type=f32)


def dot_rows(a, b):
    return lax.dot_general(a, b, (((0,), (0,)), ((), ())), preferred_element_type=f32)


def dot_cols(a, b):
    return lax.dot_general(a, b, (((1,), (1,)), ((), ())), preferred_element_type=f32)


def dot_small(a, b):
    return lax.dot_general(
        a, b, (((1,), (0,)), ((), ())), precision=lax.Precision.HIGHEST,
        preferred_element_type=f32,
    )


def mix_kernel(a00, a01, a10, a11, h00, h01, h10, h11, e0, e1, w0, w1, pick, rows_ref, scale_ref):
    wide = h00.shape[1]
    row, col = iota((64, 64), 0), iota((64, 64), 1)
    same = (row >> 4) == (col >> 4)
    outs = []
    for b, (one, two, old_one, old_two, errors) in enumerate(
        ((a00, a01, h00, h01, e0), (a10, a11, h10, h11, e1))
    ):
        lanes = one[:, wide : wide + 128].astype(f32)
        scale = jnp.where(same, lanes[:, 0:1] + lanes[:, 1:2], 0.0)
        first, second = one[:, 0:wide], two[:, 0:wide]
        gram = dot_cols(first, old_one[...]) + dot_cols(second, old_two[...])
        out = dot(first, w0[...]) + dot(second, w1[...])
        out = out + dot((scale * gram).astype(bf16), errors[...])
        scale_ref[64 * b : 64 * b + 64, :] = scale
        outs.append(out.astype(bf16))
    rows_ref[...] = dot(pick[...], jnp.concatenate(outs, axis=0)).astype(bf16)


def mix(two, hidden, errors, weights, pick):
    at = ((0, 0), (0, 1), (1, 0), (1, 1))
    width = weights[0].shape[1]
    return pl.pallas_call(
        mix_kernel,
        out_shape=(
            jax.ShapeDtypeStruct((128, width), bf16),
            jax.ShapeDtypeStruct((128, 64), f32),
        ),
        compiler_params=pltpu.CompilerParams(vmem_limit_bytes=24 * 1024 * 1024),
        cost_estimate=pl.CostEstimate(flops=600000000, bytes_accessed=4200000, transcendentals=0),
    )(*[two[k] for k in at], *[hidden[k] for k in at], *errors, *weights, pick)


def iota(shape, dim):
    return lax.broadcasted_iota(jnp.int32, shape, dim)


def per_device(inputs, targets, w_in, w_out):
    wide = w_in.shape[1]
    width = w_in.shape[0]
    groups = 16
    zh, core = lax.axis_index("zh"), lax.axis_index("c")
    xh, xl, zl = lax.axis_index("xh"), lax.axis_index("xl"), lax.axis_index("zl")
    keep = xl == 0

    def in_order(own, other):
        return jnp.where(keep, own, other), jnp.where(keep, other, own)

    both = jnp.concatenate([inputs[:, 0, :], targets[:, 0, :]], axis=0).reshape(16, 2, width)
    mine = jnp.where(core == 0, both[:, 0], both[:, 1])
    theirs = jnp.where(core == 0, both[:, 1], both[:, 0])
    theirs = swap(theirs, "c")
    pair = jnp.concatenate([mine[0:8], theirs[0:8], mine[8:16], theirs[8:16]], axis=0)
    other = swap(pair, "zh")
    wanted = jnp.concatenate([pair[16:32], other[16:32]], axis=0).astype(f32)
    every = jnp.concatenate([pair[0:16], other[0:16]], axis=0)
    every = exchange(jnp.broadcast_to(every[None], (4, 32, width)), "y").reshape(128, width)

    w_in_b = w_in.astype(bf16)
    w_out_b = w_out.astype(bf16)
    weights_in = in_order(w_in_b, swap(w_in_b, "c"))
    weights_out = in_order(w_out_b, swap(w_out_b, "c"))

    row, col = iota((128, 128), 0), iota((128, 128), 1)
    token = ((col >> 5) << 2) | ((((col >> 4) & 1) ^ zh) << 1) | (((col >> 3) & 1) ^ core)
    group = (((row >> 4) & 3) ^ zl) << 1 | ((row >> 6) ^ xh)
    pick = ((token == (row & 15)) & ((col & 7) == group)).astype(bf16)
    token = ((row >> 5) << 2) | ((((row >> 4) & 1) ^ zh) << 1) | (((row >> 3) & 1) ^ core)
    group = (((col >> 4) & 3) ^ zl) << 1 | ((col >> 6) ^ xh)
    unpick = ((token == (col & 15)) & ((row & 7) == group)).astype(bf16)

    row, col = iota((64, 64), 0), iota((64, 64), 1)
    same = (row >> 4) == (col >> 4)
    row, col = iota((64, 128), 0), iota((64, 128), 1)
    fold = ((row & 15) == col).astype(bf16)

    def with_gram(product, gram):
        lanes = dot(jnp.where(same, gram, 0.0).astype(bf16), fold)
        return jnp.concatenate([product, lanes], axis=1)

    def residuals(rows):
        moved = exchange(rows.reshape(4, 32, width), "y")
        total = jnp.sum(moved.astype(f32), axis=0)
        other = swap(total, "zh")
        total = total + jnp.concatenate([other[16:32], other[0:16]], axis=0)
        own = (total - wanted).astype(bf16)
        every = exchange(jnp.broadcast_to(own[None], (4, 32, width)), "y").reshape(128, width)
        rows = dot(pick, every).astype(bf16)
        return rows[0:64], rows[64:128]

    order = ((1, 0), (0, 1), (1, 1), (0, 0))
    features = dot(pick, every).astype(bf16)
    features = features[0:64], features[64:128]
    grams = [dot_cols(v, v) for v in features]
    pre_ext = scatter_z(
        scatter_x({(b, k): with_gram(dot(features[b], weights_in[k]), grams[b]) for b, k in order})
    )
    pre, gram_in = pre_ext[:, 0:wide], pre_ext[:, wide : wide + 16]
    hidden_own = gelu_value(pre).astype(bf16)
    hidden = gather_group(hidden_own)
    parts = [dot(hidden[b, 0], weights_out[0]) + dot(hidden[b, 1], weights_out[1]) for b in (0, 1)]
    parts = jnp.concatenate([v.astype(bf16) for v in parts], axis=0)
    errors = residuals(dot(unpick, parts).astype(bf16))
    grams = [dot_cols(v, v) for v in errors]
    back_ext = scatter_z(
        scatter_x(
            {(b, k): with_gram(dot_cols(errors[b], weights_out[k]), grams[b]) for b, k in order}
        )
    )
    back, gram_errors = back_ext[:, 0:wide], back_ext[:, wide : wide + 16]
    slopes_f = (back * gelu_slope(pre)).astype(bf16).astype(f32)
    hidden_f = hidden_own.astype(f32)
    shift = dot_small(gram_in, slopes_f)
    squares = jnp.sum(shift * slopes_f + dot_small(gram_errors, hidden_f) * hidden_f)
    squares = exchange(jnp.full((16, 8, 128), squares), ("xl", "y", "zh"))
    squares = jnp.sum(squares, axis=0)
    radius = lax.rsqrt(squares + 1e-12)[0:1, 0:1]
    pre_two = pre + radius * shift
    hidden_two_own = gelu_value(pre_two).astype(bf16)
    radius_high = radius.astype(bf16)
    radius_low = (radius - radius_high.astype(f32)).astype(bf16)
    tail = jnp.where(iota((16, 128), 1) == 0, radius_high, radius_low)
    two = gather_group(jnp.concatenate([hidden_two_own, tail], axis=1))
    hidden_two = {at: v[:, 0:wide] for at, v in two.items()}
    rows, scaled = mix(two, hidden, errors, weights_out, unpick)
    scaled = scaled[0:64], scaled[64:128]
    errors_two = residuals(rows)
    mixed = [(scaled[b] * dot_cols(errors_two[b], errors[b])).astype(bf16) for b in (0, 1)]
    total = scatter_x(
        {
            (b, k): dot_cols(errors_two[b], weights_out[k]) + dot(mixed[b], hidden[b, k])
            for b, k in order
        }
    )

    def rows_of(parts):
        first, second = (jnp.concatenate([parts[0, k], parts[1, k]], axis=0) for k in (0, 1))
        return in_order(first, second)

    features = jnp.concatenate(features, axis=0)
    errors_two = jnp.concatenate(errors_two, axis=0)
    errors_two = lax.optimization_barrier((total, errors_two))[1]
    own, other = rows_of(hidden_two)
    other = swap(dot_rows(other, errors_two).astype(bf16), "c")
    slopes_two = (scatter_z(total) * gelu_slope(pre_two)).astype(bf16)
    slopes_two, other = lax.optimization_barrier((slopes_two, other))
    slopes_two = gather_group(slopes_two)
    grad_out = (dot_rows(own, errors_two) + other.astype(f32)) / groups
    own, other = rows_of(slopes_two)
    other = swap(dot_rows(features, other).astype(bf16), "c")
    grad_in = (dot_rows(features, own) + other.astype(f32)) / groups
    return grad_in, grad_out


def solution(mesh):
    fine = Mesh(mesh.devices.reshape(4, 2, 2, 4, 2, 2), ("zl", "xh", "xl", "y", "zh", "c"))
    group, ingroup = ("zl", "xh", "xl"), ("y", "zh", "c")
    return jax.shard_map(
        per_device,
        mesh=fine,
        in_specs=(
            P(None, ingroup, group),
            P(None, ingroup, group),
            P(group, ingroup),
            P(ingroup, group),
        ),
        out_specs=(P(group, ingroup), P(ingroup, group)),
        check_vma=False,
    )
```

```python
import functools

import jax
import jax.numpy as jnp
from jax import lax
from jax.experimental import pallas as pl
from jax.experimental.pallas import tpu as pltpu
from jax.sharding import Mesh, PartitionSpec as P

root_half = 0.7071067811865476
inv_root_tau = 0.3989422804014327
bf16 = jnp.bfloat16
f32 = jnp.float32


def gelu_value(values):
    return 0.5 * values * (1.0 + lax.erf(values * root_half))


def gelu_slope(values):
    return (
        0.5 * (1.0 + lax.erf(values * root_half))
        + values * jnp.exp(-0.5 * values * values) * inv_root_tau
    )


def swap(value, axis):
    return lax.ppermute(value, axis, [(0, 1), (1, 0)])


def swap_x(value, b, k):
    pairs = [(n, n ^ (2 * b + k)) for n in range(4)]
    return lax.ppermute(value, ("xh", "xl"), pairs)


def exchange(value, axis):
    return lax.all_to_all(value, axis, 0, 0, tiled=False)


def swap_z(value, a):
    return lax.ppermute(value, "zl", [(n, n ^ a) for n in range(4)])


def scatter_x(pieces):
    moved = [swap_x(pieces[b, k].astype(bf16), b, k) for b, k in ((1, 0), (0, 1), (1, 1))]
    return pieces[0, 0] + moved[1].astype(f32) + moved[2].astype(f32) + moved[0].astype(f32)


def scatter_z(total):
    own = total[0:16]
    moved = {a: swap_z(total[16 * a : 16 * a + 16].astype(bf16), a) for a in (3, 2, 1)}
    return own + moved[1].astype(f32) + moved[2].astype(f32) + moved[3].astype(f32)


def gather_group(own):
    piece = jnp.concatenate([own] + [swap_z(own, a) for a in (1, 2, 3)], axis=0)
    moved = {(b, k): swap_x(piece, b, k) for b, k in ((1, 0), (0, 1), (1, 1))}
    moved[0, 0] = piece
    return moved


def dot(a, b):
    return lax.dot_general(a, b, (((1,), (0,)), ((), ())), preferred_element_type=f32)


def dot_rows(a, b):
    return lax.dot_general(a, b, (((0,), (0,)), ((), ())), preferred_element_type=f32)


def dot_cols(a, b):
    return lax.dot_general(a, b, (((1,), (1,)), ((), ())), preferred_element_type=f32)


def dot_small(a, b):
    return lax.dot_general(
        a, b, (((1,), (0,)), ((), ())), precision=lax.Precision.HIGHEST,
        preferred_element_type=f32,
    )


def mix_kernel(a00, a01, a10, a11, h00, h01, h10, h11, e0, e1, w0, w1, pick, rows_ref, scale_ref):
    wide = h00.shape[1]
    row, col = iota((64, 64), 0), iota((64, 64), 1)
    same = (row >> 4) == (col >> 4)
    outs = []
    for b, (one, two, old_one, old_two, errors) in enumerate(
        ((a00, a01, h00, h01, e0), (a10, a11, h10, h11, e1))
    ):
        lanes = one[:, wide : wide + 128].astype(f32)
        scale = jnp.where(same, lanes[:, 0:1] + lanes[:, 1:2], 0.0)
        first, second = one[:, 0:wide], two[:, 0:wide]
        gram = dot_cols(first, old_one[...]) + dot_cols(second, old_two[...])
        out = dot(first, w0[...]) + dot(second, w1[...])
        out = out + dot((scale * gram).astype(bf16), errors[...])
        scale_ref[64 * b : 64 * b + 64, :] = scale
        outs.append(out.astype(bf16))
    rows_ref[...] = dot(pick[...], jnp.concatenate(outs, axis=0)).astype(bf16)


def mix(two, hidden, errors, weights, pick):
    at = ((0, 0), (0, 1), (1, 0), (1, 1))
    width = weights[0].shape[1]
    return pl.pallas_call(
        mix_kernel,
        out_shape=(
            jax.ShapeDtypeStruct((128, width), bf16),
            jax.ShapeDtypeStruct((128, 64), f32),
        ),
        compiler_params=pltpu.CompilerParams(vmem_limit_bytes=24 * 1024 * 1024),
        cost_estimate=pl.CostEstimate(flops=600000000, bytes_accessed=4200000, transcendentals=0),
    )(*[two[k] for k in at], *[hidden[k] for k in at], *errors, *weights, pick)


def back_kernel(mixing, every, pick, w0, w1, *refs):
    wide = w0.shape[0]
    row, col = iota((64, 64), 0), iota((64, 64), 1)
    same = (row >> 4) == (col >> 4)
    if mixing:
        old, scale, h00, h01, h10, h11, errors_ref, own, p01, p10, p11 = refs
        hidden = ((h00, h01), (h10, h11))
    else:
        errors_ref, own, p01, p10, p11 = refs
        fold = ((iota((64, 128), 0) & 15) == iota((64, 128), 1)).astype(bf16)
    errors = dot(pick[...], every[...]).astype(bf16)
    errors_ref[...] = errors
    for b, parts in ((1, (p10, p11)), (0, (own, p01))):
        rows = errors[64 * b : 64 * b + 64]
        if mixing:
            mixed = scale[64 * b : 64 * b + 64, :] * dot_cols(rows, old[64 * b : 64 * b + 64, :])
            mixed = mixed.astype(bf16)
        for k, weights in ((0, w0), (1, w1)):
            value = dot_cols(rows, weights[...])
            if mixing:
                value = value + dot(mixed, hidden[b][k][...])
            parts[k][:, 0:wide] = value.astype(parts[k].dtype)
            if not mixing:
                lanes = dot(jnp.where(same, dot_cols(rows, rows), 0.0).astype(bf16), fold)
                parts[k][:, wide : wide + 128] = lanes.astype(parts[k].dtype)


def back_product(every, pick, weights, others):
    mixing = len(others) > 0
    wide, width = weights[0].shape
    wide = wide if mixing else wide + 128
    errors, own, p01, p10, p11 = pl.pallas_call(
        functools.partial(back_kernel, mixing),
        out_shape=(
            jax.ShapeDtypeStruct((128, width), bf16),
            jax.ShapeDtypeStruct((64, wide), f32),
            jax.ShapeDtypeStruct((64, wide), bf16),
            jax.ShapeDtypeStruct((64, wide), bf16),
            jax.ShapeDtypeStruct((64, wide), bf16),
        ),
        compiler_params=pltpu.CompilerParams(vmem_limit_bytes=24 * 1024 * 1024),
        cost_estimate=pl.CostEstimate(flops=400000000, bytes_accessed=4000000, transcendentals=0),
    )(every, pick, *weights, *others)
    return errors, {(0, 0): own, (0, 1): p01, (1, 0): p10, (1, 1): p11}


def iota(shape, dim):
    return lax.broadcasted_iota(jnp.int32, shape, dim)


def per_device(inputs, targets, w_in, w_out):
    wide = w_in.shape[1]
    width = w_in.shape[0]
    groups = 16
    zh, core = lax.axis_index("zh"), lax.axis_index("c")
    xh, xl, zl = lax.axis_index("xh"), lax.axis_index("xl"), lax.axis_index("zl")
    keep = xl == 0

    def in_order(own, other):
        return jnp.where(keep, own, other), jnp.where(keep, other, own)

    both = jnp.concatenate([inputs[:, 0, :], targets[:, 0, :]], axis=0).reshape(16, 2, width)
    mine = jnp.where(core == 0, both[:, 0], both[:, 1])
    theirs = jnp.where(core == 0, both[:, 1], both[:, 0])
    theirs = swap(theirs, "c")
    pair = jnp.concatenate([mine[0:8], theirs[0:8], mine[8:16], theirs[8:16]], axis=0)
    other = swap(pair, "zh")
    wanted = jnp.concatenate([pair[16:32], other[16:32]], axis=0).astype(f32)
    every = jnp.concatenate([pair[0:16], other[0:16]], axis=0)
    every = exchange(jnp.broadcast_to(every[None], (4, 32, width)), "y").reshape(128, width)

    w_in_b = w_in.astype(bf16)
    w_out_b = w_out.astype(bf16)
    weights_in = in_order(w_in_b, swap(w_in_b, "c"))
    weights_out = in_order(w_out_b, swap(w_out_b, "c"))

    row, col = iota((128, 128), 0), iota((128, 128), 1)
    token = ((col >> 5) << 2) | ((((col >> 4) & 1) ^ zh) << 1) | (((col >> 3) & 1) ^ core)
    group = (((row >> 4) & 3) ^ zl) << 1 | ((row >> 6) ^ xh)
    pick = ((token == (row & 15)) & ((col & 7) == group)).astype(bf16)
    token = ((row >> 5) << 2) | ((((row >> 4) & 1) ^ zh) << 1) | (((row >> 3) & 1) ^ core)
    group = (((col >> 4) & 3) ^ zl) << 1 | ((col >> 6) ^ xh)
    unpick = ((token == (col & 15)) & ((row & 7) == group)).astype(bf16)

    row, col = iota((64, 64), 0), iota((64, 64), 1)
    same = (row >> 4) == (col >> 4)
    row, col = iota((64, 128), 0), iota((64, 128), 1)
    fold = ((row & 15) == col).astype(bf16)

    def with_gram(product, gram):
        lanes = dot(jnp.where(same, gram, 0.0).astype(bf16), fold)
        return jnp.concatenate([product, lanes], axis=1)

    def residuals(rows):
        moved = exchange(rows.reshape(4, 32, width), "y")
        total = jnp.sum(moved.astype(f32), axis=0)
        other = swap(total, "zh")
        total = total + jnp.concatenate([other[16:32], other[0:16]], axis=0)
        own = (total - wanted).astype(bf16)
        return exchange(jnp.broadcast_to(own[None], (4, 32, width)), "y").reshape(128, width)

    order = ((1, 0), (0, 1), (1, 1), (0, 0))
    features = dot(pick, every).astype(bf16)
    features = features[0:64], features[64:128]
    grams = [dot_cols(v, v) for v in features]
    pre_ext = scatter_z(
        scatter_x({(b, k): with_gram(dot(features[b], weights_in[k]), grams[b]) for b, k in order})
    )
    pre, gram_in = pre_ext[:, 0:wide], pre_ext[:, wide : wide + 16]
    hidden_own = gelu_value(pre).astype(bf16)
    hidden = gather_group(hidden_own)
    parts = [dot(hidden[b, 0], weights_out[0]) + dot(hidden[b, 1], weights_out[1]) for b in (0, 1)]
    parts = jnp.concatenate([v.astype(bf16) for v in parts], axis=0)
    errors, pieces = back_product(residuals(dot(unpick, parts).astype(bf16)), pick, weights_out, ())
    back_ext = scatter_z(scatter_x(pieces))
    back, gram_errors = back_ext[:, 0:wide], back_ext[:, wide : wide + 16]
    slopes_f = (back * gelu_slope(pre)).astype(bf16).astype(f32)
    hidden_f = hidden_own.astype(f32)
    shift = dot_small(gram_in, slopes_f)
    squares = jnp.sum(shift * slopes_f + dot_small(gram_errors, hidden_f) * hidden_f)
    squares = exchange(jnp.full((16, 8, 128), squares), ("xl", "y", "zh"))
    squares = jnp.sum(squares, axis=0)
    radius = lax.rsqrt(squares + 1e-12)[0:1, 0:1]
    pre_two = pre + radius * shift
    hidden_two_own = gelu_value(pre_two).astype(bf16)
    radius_high = radius.astype(bf16)
    radius_low = (radius - radius_high.astype(f32)).astype(bf16)
    tail = jnp.where(iota((16, 128), 1) == 0, radius_high, radius_low)
    two = gather_group(jnp.concatenate([hidden_two_own, tail], axis=1))
    rows, scaled = mix(two, hidden, (errors[0:64], errors[64:128]), weights_out, unpick)
    errors_two, pieces = back_product(
        residuals(rows),
        pick,
        weights_out,
        (errors, scaled, hidden[0, 0], hidden[0, 1], hidden[1, 0], hidden[1, 1]),
    )
    total = scatter_x(pieces)

    def rows_of(parts):
        first, second = (jnp.concatenate([parts[0, k], parts[1, k]], axis=0) for k in (0, 1))
        return in_order(first, second)

    features = jnp.concatenate(features, axis=0)
    _, errors_two, two = lax.optimization_barrier((total, errors_two, two))
    own, other = rows_of({at: v[:, 0:wide] for at, v in two.items()})
    other = swap(dot_rows(other, errors_two).astype(bf16), "c")
    slopes_two = (scatter_z(total) * gelu_slope(pre_two)).astype(bf16)
    slopes_two, other = lax.optimization_barrier((slopes_two, other))
    slopes_two = gather_group(slopes_two)
    grad_out = (dot_rows(own, errors_two) + other.astype(f32)) / groups
    own, other = rows_of(slopes_two)
    other = swap(dot_rows(features, other).astype(bf16), "c")
    grad_in = (dot_rows(features, own) + other.astype(f32)) / groups
    return grad_in, grad_out


def solution(mesh):
    fine = Mesh(mesh.devices.reshape(4, 2, 2, 4, 2, 2), ("zl", "xh", "xl", "y", "zh", "c"))
    group, ingroup = ("zl", "xh", "xl"), ("y", "zh", "c")
    return jax.shard_map(
        per_device,
        mesh=fine,
        in_specs=(
            P(None, ingroup, group),
            P(None, ingroup, group),
            P(group, ingroup),
            P(ingroup, group),
        ),
        out_specs=(P(group, ingroup), P(ingroup, group)),
        check_vma=False,
    )
```

```python
import functools

import jax
import jax.numpy as jnp
from jax import lax
from jax.experimental import pallas as pl
from jax.experimental.pallas import tpu as pltpu
from jax.sharding import Mesh, PartitionSpec as P

root_half = 0.7071067811865476
inv_root_tau = 0.3989422804014327
bf16 = jnp.bfloat16
f32 = jnp.float32


def gelu_value(values):
    return 0.5 * values * (1.0 + lax.erf(values * root_half))


def gelu_slope(values):
    return (
        0.5 * (1.0 + lax.erf(values * root_half))
        + values * jnp.exp(-0.5 * values * values) * inv_root_tau
    )


def swap(value, axis):
    return lax.ppermute(value, axis, [(0, 1), (1, 0)])


def swap_x(value, b, k):
    pairs = [(n, n ^ (2 * b + k)) for n in range(4)]
    return lax.ppermute(value, ("xh", "xl"), pairs)


def exchange(value, axis):
    return lax.all_to_all(value, axis, 0, 0, tiled=False)


def swap_z(value, a):
    return lax.ppermute(value, "zl", [(n, n ^ a) for n in range(4)])


def scatter_x(pieces):
    moved = [swap_x(pieces[b, k].astype(bf16), b, k) for b, k in ((1, 0), (0, 1), (1, 1))]
    return pieces[0, 0] + moved[1].astype(f32) + moved[2].astype(f32) + moved[0].astype(f32)


def scatter_z(total):
    own = total[0:16]
    moved = {a: swap_z(total[16 * a : 16 * a + 16].astype(bf16), a) for a in (3, 2, 1)}
    return own + moved[1].astype(f32) + moved[2].astype(f32) + moved[3].astype(f32)


def gather_group(own):
    piece = jnp.concatenate([own] + [swap_z(own, a) for a in (1, 2, 3)], axis=0)
    moved = {(b, k): swap_x(piece, b, k) for b, k in ((1, 0), (0, 1), (1, 1))}
    moved[0, 0] = piece
    return moved


def dot(a, b):
    return lax.dot_general(a, b, (((1,), (0,)), ((), ())), preferred_element_type=f32)


def dot_rows(a, b):
    return lax.dot_general(a, b, (((0,), (0,)), ((), ())), preferred_element_type=f32)


def dot_cols(a, b):
    return lax.dot_general(a, b, (((1,), (1,)), ((), ())), preferred_element_type=f32)


def dot_small(a, b):
    return lax.dot_general(
        a, b, (((1,), (0,)), ((), ())), precision=lax.Precision.HIGHEST,
        preferred_element_type=f32,
    )


def mix_kernel(a00, a01, a10, a11, h00, h01, h10, h11, e0, e1, w0, w1, pick, rows_ref, scale_ref):
    wide = h00.shape[1]
    row, col = iota((64, 64), 0), iota((64, 64), 1)
    same = (row >> 4) == (col >> 4)
    outs = []
    for b, (one, two, old_one, old_two, errors) in enumerate(
        ((a00, a01, h00, h01, e0), (a10, a11, h10, h11, e1))
    ):
        lanes = one[:, wide : wide + 128].astype(f32)
        scale = jnp.where(same, lanes[:, 0:1] + lanes[:, 1:2], 0.0)
        first, second = one[:, 0:wide], two[:, 0:wide]
        gram = dot_cols(first, old_one[...]) + dot_cols(second, old_two[...])
        out = dot(first, w0[...]) + dot(second, w1[...])
        out = out + dot((scale * gram).astype(bf16), errors[...])
        scale_ref[64 * b : 64 * b + 64, :] = scale
        outs.append(out.astype(bf16))
    rows_ref[...] = dot(pick[...], jnp.concatenate(outs, axis=0)).astype(bf16)


def mix(two, hidden, errors, weights, pick):
    at = ((0, 0), (0, 1), (1, 0), (1, 1))
    width = weights[0].shape[1]
    return pl.pallas_call(
        mix_kernel,
        out_shape=(
            jax.ShapeDtypeStruct((128, width), bf16),
            jax.ShapeDtypeStruct((128, 64), f32),
        ),
        compiler_params=pltpu.CompilerParams(vmem_limit_bytes=24 * 1024 * 1024),
        cost_estimate=pl.CostEstimate(flops=600000000, bytes_accessed=4200000, transcendentals=0),
    )(*[two[k] for k in at], *[hidden[k] for k in at], *errors, *weights, pick)


def step_kernel(parts, pre, shift, both_ref, pre_two_ref):
    wide = shift.shape[1]
    radius = lax.rsqrt(jnp.sum(parts[...], axis=0) + 1e-12)[0:1, 0:1]
    pre_two = pre[:, 0:wide] + radius * shift[...]
    pre_two_ref[...] = pre_two
    both_ref[:, 0:wide] = gelu_value(pre_two).astype(bf16)
    high = radius.astype(bf16).astype(f32)
    lane = iota((16, 128), 1)
    both_ref[:, wide : wide + 128] = jnp.where(lane == 0, high, radius - high).astype(bf16)


def perturbed(parts, pre_ext, shift):
    wide = shift.shape[1]
    return pl.pallas_call(
        step_kernel,
        out_shape=(
            jax.ShapeDtypeStruct((16, wide + 128), bf16),
            jax.ShapeDtypeStruct((16, wide), f32),
        ),
        compiler_params=pltpu.CompilerParams(vmem_limit_bytes=8 * 1024 * 1024),
        cost_estimate=pl.CostEstimate(flops=1000000, bytes_accessed=400000, transcendentals=25000),
    )(parts, pre_ext, shift)


def back_kernel(mixing, every, pick, w0, w1, *refs):
    wide = w0.shape[0]
    row, col = iota((64, 64), 0), iota((64, 64), 1)
    same = (row >> 4) == (col >> 4)
    if mixing:
        old, scale, h00, h01, h10, h11, errors_ref, own, p01, p10, p11 = refs
        hidden = ((h00, h01), (h10, h11))
    else:
        errors_ref, own, p01, p10, p11 = refs
        fold = ((iota((64, 128), 0) & 15) == iota((64, 128), 1)).astype(bf16)
    errors = dot(pick[...], every[...]).astype(bf16)
    errors_ref[...] = errors
    for b, parts in ((1, (p10, p11)), (0, (own, p01))):
        rows = errors[64 * b : 64 * b + 64]
        if mixing:
            mixed = scale[64 * b : 64 * b + 64, :] * dot_cols(rows, old[64 * b : 64 * b + 64, :])
            mixed = mixed.astype(bf16)
        for k, weights in ((0, w0), (1, w1)):
            value = dot_cols(rows, weights[...])
            if mixing:
                value = value + dot(mixed, hidden[b][k][...])
            parts[k][:, 0:wide] = value.astype(parts[k].dtype)
            if not mixing:
                lanes = dot(jnp.where(same, dot_cols(rows, rows), 0.0).astype(bf16), fold)
                parts[k][:, wide : wide + 128] = lanes.astype(parts[k].dtype)


def back_product(every, pick, weights, others):
    mixing = len(others) > 0
    wide, width = weights[0].shape
    wide = wide if mixing else wide + 128
    errors, own, p01, p10, p11 = pl.pallas_call(
        functools.partial(back_kernel, mixing),
        out_shape=(
            jax.ShapeDtypeStruct((128, width), bf16),
            jax.ShapeDtypeStruct((64, wide), f32),
            jax.ShapeDtypeStruct((64, wide), bf16),
            jax.ShapeDtypeStruct((64, wide), bf16),
            jax.ShapeDtypeStruct((64, wide), bf16),
        ),
        compiler_params=pltpu.CompilerParams(vmem_limit_bytes=24 * 1024 * 1024),
        cost_estimate=pl.CostEstimate(flops=400000000, bytes_accessed=4000000, transcendentals=0),
    )(every, pick, *weights, *others)
    return errors, {(0, 0): own, (0, 1): p01, (1, 0): p10, (1, 1): p11}


def iota(shape, dim):
    return lax.broadcasted_iota(jnp.int32, shape, dim)


def per_device(inputs, targets, w_in, w_out):
    wide = w_in.shape[1]
    width = w_in.shape[0]
    groups = 16
    zh, core = lax.axis_index("zh"), lax.axis_index("c")
    xh, xl, zl = lax.axis_index("xh"), lax.axis_index("xl"), lax.axis_index("zl")
    keep = xl == 0

    def in_order(own, other):
        return jnp.where(keep, own, other), jnp.where(keep, other, own)

    both = jnp.concatenate([inputs[:, 0, :], targets[:, 0, :]], axis=0).reshape(16, 2, width)
    mine = jnp.where(core == 0, both[:, 0], both[:, 1])
    theirs = jnp.where(core == 0, both[:, 1], both[:, 0])
    theirs = swap(theirs, "c")
    pair = jnp.concatenate([mine[0:8], theirs[0:8], mine[8:16], theirs[8:16]], axis=0)
    other = swap(pair, "zh")
    wanted = jnp.concatenate([pair[16:32], other[16:32]], axis=0).astype(f32)
    every = jnp.concatenate([pair[0:16], other[0:16]], axis=0)
    every = exchange(jnp.broadcast_to(every[None], (4, 32, width)), "y").reshape(128, width)

    w_in_b = w_in.astype(bf16)
    w_out_b = w_out.astype(bf16)
    weights_in = in_order(w_in_b, swap(w_in_b, "c"))
    weights_out = in_order(w_out_b, swap(w_out_b, "c"))

    row, col = iota((128, 128), 0), iota((128, 128), 1)
    token = ((col >> 5) << 2) | ((((col >> 4) & 1) ^ zh) << 1) | (((col >> 3) & 1) ^ core)
    group = (((row >> 4) & 3) ^ zl) << 1 | ((row >> 6) ^ xh)
    pick = ((token == (row & 15)) & ((col & 7) == group)).astype(bf16)
    token = ((row >> 5) << 2) | ((((row >> 4) & 1) ^ zh) << 1) | (((row >> 3) & 1) ^ core)
    group = (((col >> 4) & 3) ^ zl) << 1 | ((col >> 6) ^ xh)
    unpick = ((token == (col & 15)) & ((row & 7) == group)).astype(bf16)

    row, col = iota((64, 64), 0), iota((64, 64), 1)
    same = (row >> 4) == (col >> 4)
    row, col = iota((64, 128), 0), iota((64, 128), 1)
    fold = ((row & 15) == col).astype(bf16)

    def with_gram(product, gram):
        lanes = dot(jnp.where(same, gram, 0.0).astype(bf16), fold)
        return jnp.concatenate([product, lanes], axis=1)

    def residuals(rows):
        moved = exchange(rows.reshape(4, 32, width), "y")
        total = jnp.sum(moved.astype(f32), axis=0)
        other = swap(total, "zh")
        total = total + jnp.concatenate([other[16:32], other[0:16]], axis=0)
        own = (total - wanted).astype(bf16)
        return exchange(jnp.broadcast_to(own[None], (4, 32, width)), "y").reshape(128, width)

    order = ((1, 0), (0, 1), (1, 1), (0, 0))
    features = dot(pick, every).astype(bf16)
    features = features[0:64], features[64:128]
    grams = [dot_cols(v, v) for v in features]
    pre_ext = scatter_z(
        scatter_x({(b, k): with_gram(dot(features[b], weights_in[k]), grams[b]) for b, k in order})
    )
    pre, gram_in = pre_ext[:, 0:wide], pre_ext[:, wide : wide + 16]
    hidden_own = gelu_value(pre).astype(bf16)
    hidden = gather_group(hidden_own)
    parts = [dot(hidden[b, 0], weights_out[0]) + dot(hidden[b, 1], weights_out[1]) for b in (0, 1)]
    parts = jnp.concatenate([v.astype(bf16) for v in parts], axis=0)
    errors, pieces = back_product(residuals(dot(unpick, parts).astype(bf16)), pick, weights_out, ())
    back_ext = scatter_z(scatter_x(pieces))
    back, gram_errors = back_ext[:, 0:wide], back_ext[:, wide : wide + 16]
    slopes_f = (back * gelu_slope(pre)).astype(bf16).astype(f32)
    hidden_f = hidden_own.astype(f32)
    shift = dot_small(gram_in, slopes_f)
    squares = jnp.sum(shift * slopes_f + dot_small(gram_errors, hidden_f) * hidden_f)
    squares = exchange(jnp.full((16, 8, 128), squares), ("xl", "y", "zh"))
    both, pre_two = perturbed(squares, pre_ext, shift)
    two = gather_group(both)
    rows, scaled = mix(two, hidden, (errors[0:64], errors[64:128]), weights_out, unpick)
    errors_two, pieces = back_product(
        residuals(rows),
        pick,
        weights_out,
        (errors, scaled, hidden[0, 0], hidden[0, 1], hidden[1, 0], hidden[1, 1]),
    )
    total = scatter_x(pieces)

    def rows_of(parts):
        first, second = (jnp.concatenate([parts[0, k], parts[1, k]], axis=0) for k in (0, 1))
        return in_order(first, second)

    features = jnp.concatenate(features, axis=0)
    _, errors_two, two = lax.optimization_barrier((total, errors_two, two))
    own, other = rows_of({at: v[:, 0:wide] for at, v in two.items()})
    other = swap(dot_rows(other, errors_two).astype(bf16), "c")
    slopes_two = (scatter_z(total) * gelu_slope(pre_two)).astype(bf16)
    slopes_two, other = lax.optimization_barrier((slopes_two, other))
    slopes_two = gather_group(slopes_two)
    grad_out = (dot_rows(own, errors_two) + other.astype(f32)) / groups
    own, other = rows_of(slopes_two)
    other = swap(dot_rows(features, other).astype(bf16), "c")
    grad_in = (dot_rows(features, own) + other.astype(f32)) / groups
    return grad_in, grad_out


def solution(mesh):
    fine = Mesh(mesh.devices.reshape(4, 2, 2, 4, 2, 2), ("zl", "xh", "xl", "y", "zh", "c"))
    group, ingroup = ("zl", "xh", "xl"), ("y", "zh", "c")
    return jax.shard_map(
        per_device,
        mesh=fine,
        in_specs=(
            P(None, ingroup, group),
            P(None, ingroup, group),
            P(group, ingroup),
            P(ingroup, group),
        ),
        out_specs=(P(group, ingroup), P(ingroup, group)),
        check_vma=False,
    )
```
